32 devices in a mesh: mode: 8 (over z, y), space: 4 (over x, core).
Axes of the slice: x: 2, y: 2, z: 4, core: 2. Of those that a mesh axis runs over, the one named last changes fastest.
Arguments:
- modes: bfloat16 [3, 256, 16, 4, 128], P(None, 'mode', 'space'), may hold values from -6 to 6
- weights: float32 [16, 4, 128], P('space'), may hold values from 0.001275776 to 0.031894397
- plan: int32 [3], replicated, may hold values from 0 to 7, as said below
Outputs:
- convection: float32 [128, 32, 256], P('space', None, 'mode')
The draws below stay inside these ranges and needn't reach their ends.
Inputs may be any that keep to these rules, and one draw needn't show every extreme that they name: plan[0] is 256 / 32 - 1, the last aligned block of 32 modes; plan[1] to plan[2] are distinct indices of aligned panels of 64 modes, below 256 / 64.
All inputs are finite; a program needn't handle non-finite values.
Results may differ from the reference program's by a relative error of at most 0.0041.
Values may be sent and summed in bfloat16 or wider, within the bound.
A program may use at most 128 MiB of HBM per device.

```python
import math
import jax
import jax.numpy as jnp
from jax import lax

M_DEV = 32
MODES = 256
PANEL = 64
NPANEL = 2
TESTS = 128
CY = 4
CZ = 128
NX = 16


def draw_plan(key, part):
    panel_key = jax.random.fold_in(key, 23)
    owner = jnp.full((1,), MODES // M_DEV - 1, dtype=jnp.int32)
    panels = jax.random.permutation(panel_key, jnp.arange(MODES // PANEL, dtype=jnp.int32))[:NPANEL]
    return jnp.concatenate([owner, panels.astype(jnp.int32)]).astype(jnp.int32)


def block_levels(own_key, dims, shards, least, high):
    loudness = 1.0
    for dim, shards_of in shards:
        steps = jax.random.uniform(jax.random.fold_in(jax.random.fold_in(own_key, 6), dim), (shards_of,), jnp.float32, least / len(shards), high / len(shards))
        loudness = loudness * jnp.repeat(jnp.exp(steps), dims[dim] // shards_of).reshape((-1,) + (1,) * (len(dims) - 1 - dim))
    return loudness


def noise(key, shape, width, most, cuts=(), held_as=jnp.bfloat16):
    array = width * jax.random.normal(key, shape, jnp.float32)
    if cuts:
        array = array * block_levels(key, shape, cuts, -0.22, 0.18)
    return jnp.clip(array, -most, most).astype(held_as)


def setup_inputs(seed: int = 0) -> dict:
    arg_keys = jax.random.split(jax.random.key(seed), 4)
    return {
        "modes": noise(arg_keys[0], (3, MODES, NX, CY, CZ), 1.0, 6.0, ((1, 8), (2, 4))),
        "weights": jnp.clip(jnp.exp(math.log(0.031894397) - 3.218876 * jax.random.uniform(arg_keys[1], (NX, CY, CZ), jnp.float32) ** block_levels(arg_keys[1], (NX, CY, CZ), ((0, 4),), -0.2, 0.2)), 0.001275776, 0.031894397),
        "plan": draw_plan(jax.random.fold_in(arg_keys[3], 71), 0),
    }


def reference(modes, weights, plan):
    advecting = lax.dynamic_slice_in_dim(modes, (plan[0] * M_DEV).astype(jnp.int32), M_DEV, 1)
    panels = [lax.dynamic_slice_in_dim(modes, (plan[1 + panel] * PANEL).astype(jnp.int32), PANEL, 1) for panel in range(NPANEL)]
    tests = jnp.concatenate(panels, axis=1)
    weighted = (weights[None, None] * tests.astype(jnp.float32)).astype(jnp.bfloat16)

    def plane_step(total, plane):
        before = jnp.mod(plane - 1, NX).astype(jnp.int32)
        after = jnp.mod(plane + 1, NX).astype(jnp.int32)
        center = lax.dynamic_index_in_dim(modes, plane, 2, keepdims=False).astype(jnp.float32)
        lower = lax.dynamic_index_in_dim(modes, before, 2, keepdims=False).astype(jnp.float32)
        upper = lax.dynamic_index_in_dim(modes, after, 2, keepdims=False).astype(jnp.float32)
        grad_x = 0.5 * (upper - lower)
        grad_y = 0.5 * (jnp.roll(center, -1, axis=2) - jnp.roll(center, 1, axis=2))
        grad_z = 0.5 * (jnp.roll(center, -1, axis=3) - jnp.roll(center, 1, axis=3))
        advect = lax.dynamic_index_in_dim(advecting, plane, 2, keepdims=False).astype(jnp.float32)
        values = advect[0][None, :, None] * grad_x[:, None]
        values = values + advect[1][None, :, None] * grad_y[:, None]
        values = values + advect[2][None, :, None] * grad_z[:, None]
        values = values.astype(jnp.bfloat16).reshape(3, M_DEV * MODES, CY * CZ)
        tested = lax.dynamic_index_in_dim(weighted, plane, 2, keepdims=False).reshape(3, TESTS, CY * CZ)
        total = total + lax.dot_general(tested, values, (((0, 2), (0, 2)), ((), ())), preferred_element_type=jnp.float32)
        return total, None

    start_total = jnp.zeros((TESTS, M_DEV * MODES), jnp.float32)
    total, unused = lax.scan(plane_step, start_total, jnp.arange(NX, dtype=jnp.int32))
    return total.reshape(TESTS, M_DEV, MODES)
```

```python
import functools

import jax
import jax.numpy as jnp
from jax import lax
from jax.experimental import pallas as pl
from jax.experimental.pallas import tpu as pltpu
from jax.sharding import PartitionSpec as P

PANEL = 64
NPANEL = 2
MESH = pl.DeviceIdType.MESH
F32 = jnp.float32
BF16 = jnp.bfloat16


def kernel(dims, plan_ref, x_ref, weights_ref, out_ref,
           pk, bd, gq, bq, wq, advf, wts, vals, acc, crx, own, xo, xi, zo, zi,
           z_send, z_recv, b_send, b_recv, y_send, y_recv, h_send, h_recv,
           c_send, c_recv, s_send, s_recv, r_send, r_recv):
    nmode, spaces = dims
    comps, nm, nx, cy, lanes = x_ref.shape
    own_rows = out_ref.shape[0]
    parts = cy
    width = lanes // parts
    units = nx * comps
    cols = nmode // parts
    half = spaces // 2
    per_panel = PANEL // nm
    mode = lax.axis_index("mode")
    me = lax.axis_index("space")
    zq = lax.rem(mode // 2, parts)
    col = (mode // (2 * parts)) * 2 + lax.rem(mode, 2)
    core = lax.rem(me, 2)
    row = me // 2
    adv_block = nmode - 1

    def member(c, z):
        return (c // 2) * (2 * parts) + z * 2 + lax.rem(c, 2)

    def to_mode(m):
        return {"device_id": {"mode": m}, "device_id_type": MESH}

    def to_space(s):
        return {"device_id": {"space": s}, "device_id_type": MESH}

    barrier = pltpu.get_barrier_semaphore()
    for d in range(1, parts):
        pl.semaphore_signal(barrier, inc=1, **to_mode(member(col, lax.rem(zq + d, parts))))
    for d in range(1, cols):
        pl.semaphore_signal(barrier, inc=1, **to_mode(member(lax.rem(col + d, cols), zq)))
    for d in range(1, spaces):
        pl.semaphore_signal(barrier, inc=1, **to_space(lax.rem(me + d, spaces)))

    lane = lax.broadcasted_iota(jnp.int32, (nm, lanes), 1)
    group, inner = lane // width, lax.rem(lane, width)

    def roll(v, shift):
        shift = shift % lanes
        return pltpu.roll(v, shift, 1) if shift else v

    edges = [jnp.zeros((nm, lanes), F32) for _ in range(parts)]
    for p in range(nx):
        for c in range(comps):
            u = p * comps + c
            rows = jnp.swapaxes(x_ref[c, :, p], 0, 1)
            rows = [rows[y].astype(F32) for y in range(cy)]
            packed = []
            for t in range(parts):
                v = roll(rows[0], -width * t)
                for y in range(1, cy):
                    v = jnp.where(group == y, roll(rows[y], width * (y - t)), v)
                packed.append(v)
                pk[t, u] = v.astype(BF16)
            for t in range(parts):
                low = roll(packed[(t - 1) % parts], 2 * u - width + 1)
                high = roll(packed[(t + 1) % parts], 2 * u + 1)
                edges[t] = jnp.where(inner == 2 * u, low, jnp.where(inner == 2 * u + 1, high, edges[t]))
    for t in range(parts):
        bd[t] = edges[t].astype(BF16)
    gq[mode, comps : comps + units] = pk[zq]
    bq[zq] = bd[zq]
    for p in range(nx):
        w = None
        for y in range(cy):
            line = jnp.broadcast_to(weights_ref[p, y : y + 1, :], (8, lanes))
            line = pltpu.roll(line, lax.rem(width * (y - zq + parts), lanes), 1)
            w = line if w is None else jnp.where(group[:8] == y, line, w)
        wq[p] = w

    pl.semaphore_wait(barrier, parts - 1 + cols - 1 + spaces - 1)

    def copy_z(d, p):
        t = lax.rem(zq + d, parts)
        return pltpu.make_async_remote_copy(
            src_ref=pk.at[t, pl.ds(p * comps, comps)], dst_ref=gq.at[mode, pl.ds((p + 1) * comps, comps)],
            send_sem=z_send.at[d - 1, p], recv_sem=z_recv.at[zq, p], **to_mode(member(col, t)))

    def got_z(z, p):
        m = member(col, z)
        return pltpu.make_async_remote_copy(
            src_ref=pk.at[0, pl.ds(p * comps, comps)], dst_ref=gq.at[m, pl.ds((p + 1) * comps, comps)],
            send_sem=z_send.at[0, p], recv_sem=z_recv.at[z, p], **to_mode(m))

    def copy_b(d):
        t = lax.rem(zq + d, parts)
        return pltpu.make_async_remote_copy(
            src_ref=bd.at[t], dst_ref=bq.at[zq],
            send_sem=b_send.at[d - 1], recv_sem=b_recv.at[zq], **to_mode(member(col, t)))

    def got_b(z):
        return pltpu.make_async_remote_copy(
            src_ref=bd.at[0], dst_ref=bq.at[z],
            send_sem=b_send.at[0], recv_sem=b_recv.at[z], **to_mode(member(col, z)))

    def copy_y(d, z, p):
        m = member(col, z)
        part = gq.at[m, pl.ds((p + 1) * comps, comps)]
        return pltpu.make_async_remote_copy(
            src_ref=part, dst_ref=part, send_sem=y_send.at[d - 1, z, p], recv_sem=y_recv.at[cols - d - 1, z, p],
            **to_mode(member(lax.rem(col + d, cols), zq)))

    def got_y(d, z, p):
        peer = lax.rem(col + d, cols)
        part = gq.at[member(peer, z), pl.ds((p + 1) * comps, comps)]
        return pltpu.make_async_remote_copy(
            src_ref=part, dst_ref=part, send_sem=y_send.at[d - 1, z, p], recv_sem=y_recv.at[d - 1, z, p],
            **to_mode(member(peer, zq)))

    def copy_h(z, side):
        m = member(col, z)
        first, there, peer = ((nx * comps, 0, me + 1), (comps, (nx + 1) * comps, me + spaces - 1))[side]
        return pltpu.make_async_remote_copy(
            src_ref=gq.at[m, pl.ds(first, comps)], dst_ref=gq.at[m, pl.ds(there, comps)],
            send_sem=h_send.at[z, side], recv_sem=h_recv.at[z, side], **to_space(lax.rem(peer, spaces)))

    def copy_c(n):
        return pltpu.make_async_remote_copy(
            src_ref=acc.at[n, 1 - core], dst_ref=crx.at[n],
            send_sem=c_send.at[n], recv_sem=c_recv.at[n], **to_space(row * 2 + 1 - core))

    def copy_s(n, d):
        peer = lax.rem(row + d, half)
        return pltpu.make_async_remote_copy(
            src_ref=xo.at[n, peer], dst_ref=xi.at[n, half - d - 1],
            send_sem=s_send.at[n, d - 1], recv_sem=s_recv.at[n, half - d - 1], **to_space(peer * 2 + core))

    def got_s(n, d):
        peer = lax.rem(row + d, half)
        return pltpu.make_async_remote_copy(
            src_ref=xo.at[n, peer], dst_ref=xi.at[n, d - 1],
            send_sem=s_send.at[n, d - 1], recv_sem=s_recv.at[n, d - 1], **to_space(peer * 2 + core))

    def copy_r(n):
        return pltpu.make_async_remote_copy(
            src_ref=zo.at[n], dst_ref=zi.at[n],
            send_sem=r_send.at[n], recv_sem=r_recv.at[n], **to_mode(member(col, lax.rem(zq + 1 + n, parts))))

    source = zq == parts - 1

    @pl.when(source)
    def _():
        for p in range(nx):
            for d in range(1, parts):
                copy_z(d, p).start()

    @pl.when(jnp.logical_not(source))
    def _():
        for d in range(1, parts):
            for p in range(nx):
                copy_z(d, p).start()

    for d in range(1, parts):
        copy_b(d).start()
    for p in range(nx):
        for d in range(1, cols):
            copy_y(d, zq, p).start()
    for side in range(2):
        copy_h(zq, side).start()

    def other(n):
        head = parts - 1 if n == 0 else lax.rem(zq - n + parts - 1, parts - 1)
        return jnp.where(source, parts - 2 - n, head)

    def forward(z):
        for p in range(nx):
            got_z(z, p).wait_recv()
            for d in range(1, cols):
                copy_y(d, z, p).start()
            if p == 0:
                copy_h(z, 1).start()
        copy_h(z, 0).start()

    def values_of(z):
        m = member(col, z)
        edge = bq[z].astype(F32)
        for side in range(2):
            copy_h(z, side).wait_recv()
        for p in range(nx):
            grads = []
            for c in range(comps):
                u = p * comps + c
                at = (p + 1) * comps + c
                center = gq[m, at].astype(F32)
                gx = 0.5 * (gq[m, at + comps].astype(F32) - gq[m, at - comps].astype(F32))
                gy = 0.5 * (roll(center, -width) - roll(center, width))
                after = jnp.where(inner == width - 1, roll(edge, width - 2 - 2 * u), roll(center, -1))
                before = jnp.where(inner == 0, roll(edge, -2 * u), roll(center, 1))
                grads.append((gx, gy, 0.5 * (after - before)))

            def line(j, carry):
                rows = [jnp.broadcast_to(advf[p, d, pl.ds(j, 1), :], (nm, lanes)) for d in range(3)]
                start = pl.multiple_of(j * nm, nm)
                for c in range(comps):
                    value = rows[0] * grads[c][0] + rows[1] * grads[c][1] + rows[2] * grads[c][2]
                    vals[z, p * comps + c, pl.ds(start, nm), :] = value.astype(BF16)
                return carry

            lax.fori_loop(0, nm, line, 0, unroll=4)

    forward(other(0))

    adv_rel = cols - 1 - col

    @pl.when(col != cols - 1)
    def _():
        for p in range(nx):
            got_y(adv_rel, parts - 1, p).wait_recv()

    for p in range(nx):
        for d in range(comps):
            advf[p, d] = gq[adv_block, (p + 1) * comps + d].astype(F32)

    values_of(zq)
    for n in range(1, parts - 1):
        forward(other(n))
        got_b(other(n - 1)).wait_recv()
        values_of(other(n - 1))
    got_b(other(parts - 2)).wait_recv()
    values_of(other(parts - 2))

    for d in range(1, cols):
        for z in range(parts):
            def rest(d=d, z=z):
                for p in range(nx):
                    got_y(d, z, p).wait_recv()
            if z == parts - 1:
                pl.when(adv_rel != d)(rest)
            else:
                rest()

    for u in range(units):
        weight = wq[u // comps, 0:1, :]
        for t in range(NPANEL):
            for r in range(per_panel):
                raw = gq[plan_ref[1 + t] * per_panel + r, comps + u].astype(F32)
                first = (t * per_panel + r) * nm
                wts[u, first : first + nm, :] = (weight * raw).astype(BF16)

    def gemm(n):
        z = lax.rem(zq + 1 + n, parts)
        left = jnp.concatenate([wts[u] for u in range(units)], axis=1)
        right = jnp.concatenate([vals[z, u] for u in range(units)], axis=1)
        part = lax.dot_general(left, right, (((1,), (1,)), ((), ())), preferred_element_type=F32)
        for s in range(spaces):
            acc[n, s % 2, s // 2] = part[s * own_rows : (s + 1) * own_rows]
        copy_c(n).start()

    def stage_s(n):
        copy_c(n).wait_recv()
        for h in range(half):
            xo[n, h] = (acc[n, core, h] + crx[n, h]).astype(BF16)
        own[n] = acc[n, core, row] + crx[n, row]
        for d in range(1, half):
            copy_s(n, d).start()

    def total(n):
        value = own[n]
        for d in range(1, half):
            got_s(n, d).wait_recv()
            value = value + xi[n, d - 1].astype(F32)
        return value

    def stage_r(n):
        zo[n] = total(n).astype(BF16)
        copy_r(n).start()

    for n in range(parts):
        gemm(n)
        if n >= 1:
            stage_s(n - 1)
        if n >= 2:
            stage_r(n - 2)
    stage_s(parts - 1)
    stage_r(parts - 2)

    result = total(parts - 1)
    for n in range(parts - 1):
        copy_r(n).wait_recv()
        result = result + zi[n].astype(F32)
    out_ref[...] = result

    for d in range(1, parts):
        for p in range(nx):
            copy_z(d, p).wait_send()
        copy_b(d).wait_send()
    for z in range(parts):
        for d in range(1, cols):
            for p in range(nx):
                copy_y(d, z, p).wait_send()
        for side in range(2):
            copy_h(z, side).wait_send()
    for n in range(parts):
        copy_c(n).wait_send()
        for d in range(1, half):
            copy_s(n, d).wait_send()
        if n < parts - 1:
            copy_r(n).wait_send()


def solution(mesh):
    nmode, spaces = mesh.shape["mode"], mesh.shape["space"]

    def local(modes, weights, plan):
        comps, nm, nx, cy, lanes = modes.shape
        parts, units = cy, comps * nx
        cols, half = nmode // parts, spaces // 2
        test_count = NPANEL * PANEL
        own_rows = test_count // spaces
        assert PANEL % nm == 0 and lanes % parts == 0 and 2 * units <= lanes // parts
        assert nmode % (2 * parts) == 0 and spaces % 2 == 0
        vm = pl.BlockSpec(memory_space=pltpu.VMEM)
        dma = pltpu.SemaphoreType.DMA
        piece = (own_rows, nm * nm)
        pairs = max(half - 1, 1)
        out = pl.pallas_call(
            functools.partial(kernel, (nmode, spaces)),
            out_shape=jax.ShapeDtypeStruct(piece, F32),
            in_specs=[pl.BlockSpec(memory_space=pltpu.SMEM), vm, vm],
            out_specs=vm,
            scratch_shapes=[
                pltpu.VMEM((parts, units, nm, lanes), BF16),
                pltpu.VMEM((parts, nm, lanes), BF16),
                pltpu.VMEM((nmode, units + 2 * comps, nm, lanes), BF16),
                pltpu.VMEM((parts, nm, lanes), BF16),
                pltpu.VMEM((nx, 8, lanes), F32),
                pltpu.VMEM((nx, comps, nm, lanes), F32),
                pltpu.VMEM((units, test_count, lanes), BF16),
                pltpu.VMEM((parts, units, nm * nm, lanes), BF16),
                pltpu.VMEM((parts, 2, half) + piece, F32),
                pltpu.VMEM((parts, half) + piece, F32),
                pltpu.VMEM((parts,) + piece, F32),
                pltpu.VMEM((parts, half) + piece, BF16),
                pltpu.VMEM((parts, pairs) + piece, BF16),
                pltpu.VMEM((parts - 1,) + piece, BF16),
                pltpu.VMEM((parts - 1,) + piece, BF16),
                dma((parts - 1, nx)), dma((parts, nx)), dma((parts - 1,)), dma((parts,)),
                dma((cols - 1, parts, nx)), dma((cols - 1, parts, nx)), dma((parts, 2)), dma((parts, 2)),
                dma((parts,)), dma((parts,)), dma((parts, pairs)), dma((parts, pairs)),
                dma((parts - 1,)), dma((parts - 1,)),
            ],
            compiler_params=pltpu.CompilerParams(
                collective_id=0, has_side_effects=True, vmem_limit_bytes=56 * 1024 * 1024),
        )(plan, modes, weights)
        return out.reshape(own_rows, nm, nm)

    in_specs = (P(None, "mode", "space", None, None), P("space", None, None), P())
    return jax.shard_map(local, mesh=mesh, in_specs=in_specs, out_specs=P("space", None, "mode"), check_vma=False)
```

```python
import functools

import jax
import jax.numpy as jnp
from jax import lax
from jax.experimental import pallas as pl
from jax.experimental.pallas import tpu as pltpu
from jax.sharding import PartitionSpec as P

PANEL = 64
NPANEL = 2
SPLIT = 2
LAG_S = 2
LAG_R = 5
MESH = pl.DeviceIdType.MESH
F32 = jnp.float32
BF16 = jnp.bfloat16


def kernel(dims, plan_ref, x_ref, weights_ref, out_ref,
           pk, bd, gq, bq, wq, advf, wts, vals, acc, cbo, crx, own, xo, xi, zo, zi, fin,
           z_send, z_recv, b_send, b_recv, y_send, y_recv, h_send, h_recv,
           c_send, c_recv, s_send, s_recv, r_send, r_recv):
    nmode, spaces = dims
    comps, nm, nx, cy, lanes = x_ref.shape
    own_rows = out_ref.shape[0] // nm
    parts = cy
    width = lanes // parts
    units = nx * comps
    cols = nmode // parts
    half = spaces // 2
    per_panel = PANEL // nm
    mode = lax.axis_index("mode")
    me = lax.axis_index("space")
    zq = lax.rem(mode // 2, parts)
    col = (mode // (2 * parts)) * 2 + lax.rem(mode, 2)
    core = lax.rem(me, 2)
    row = me // 2
    adv_block = nmode - 1
    planes = list(range(1, nx - 1)) + [0, nx - 1]
    steps = parts * SPLIT
    span = nm * nm // SPLIT

    def member(c, z):
        return (c // 2) * (2 * parts) + z * 2 + lax.rem(c, 2)

    def to_mode(m):
        return {"device_id": {"mode": m}, "device_id_type": MESH}

    def to_space(s):
        return {"device_id": {"space": s}, "device_id_type": MESH}

    barrier = pltpu.get_barrier_semaphore()
    for d in range(1, parts):
        pl.semaphore_signal(barrier, inc=1, **to_mode(member(col, lax.rem(zq + d, parts))))
    for d in range(1, cols):
        pl.semaphore_signal(barrier, inc=1, **to_mode(member(lax.rem(col + d, cols), zq)))
    for d in range(1, spaces):
        pl.semaphore_signal(barrier, inc=1, **to_space(lax.rem(me + d, spaces)))

    lane = lax.broadcasted_iota(jnp.int32, (nm, lanes), 1)
    group, inner = lane // width, lax.rem(lane, width)

    def roll(v, shift):
        shift = shift % lanes
        return pltpu.roll(v, shift, 1) if shift else v

    for p in range(nx):
        for c in range(comps):
            u = p * comps + c
            rows = jnp.swapaxes(x_ref[c, :, p], 0, 1)
            rows = [rows[y].astype(F32) for y in range(cy)]
            for t in range(parts):
                v = roll(rows[0], -width * t)
                for y in range(1, cy):
                    v = jnp.where(group == y, roll(rows[y], width * (y - t)), v)
                pk[t, u] = v.astype(BF16)
    gq[mode, comps : comps + units] = pk[zq]
    for p in range(nx):
        w = None
        for y in range(cy):
            line = jnp.broadcast_to(weights_ref[p, y : y + 1, :], (8, lanes))
            line = pltpu.roll(line, lax.rem(width * (y - zq + parts), lanes), 1)
            w = line if w is None else jnp.where(group[:8] == y, line, w)
        wq[p] = w

    pl.semaphore_wait(barrier, parts - 1 + cols - 1 + spaces - 1)

    def copy_z(t, p):
        return pltpu.make_async_remote_copy(
            src_ref=pk.at[t, pl.ds(p * comps, comps)], dst_ref=gq.at[mode, pl.ds((p + 1) * comps, comps)],
            send_sem=z_send.at[t, p], recv_sem=z_recv.at[zq, p], **to_mode(member(col, t)))

    def got_z(z, p):
        m = member(col, z)
        return pltpu.make_async_remote_copy(
            src_ref=pk.at[0, pl.ds(p * comps, comps)], dst_ref=gq.at[m, pl.ds((p + 1) * comps, comps)],
            send_sem=z_send.at[0, p], recv_sem=z_recv.at[z, p], **to_mode(m))

    def copy_b(d):
        t = lax.rem(zq + d, parts)
        return pltpu.make_async_remote_copy(
            src_ref=bd.at[t], dst_ref=bq.at[zq],
            send_sem=b_send.at[d - 1], recv_sem=b_recv.at[zq], **to_mode(member(col, t)))

    def got_b(z):
        return pltpu.make_async_remote_copy(
            src_ref=bd.at[0], dst_ref=bq.at[z],
            send_sem=b_send.at[0], recv_sem=b_recv.at[z], **to_mode(member(col, z)))

    def copy_y(d, z, p):
        m = member(col, z)
        part = gq.at[m, pl.ds((p + 1) * comps, comps)]
        return pltpu.make_async_remote_copy(
            src_ref=part, dst_ref=part, send_sem=y_send.at[d - 1, z, p], recv_sem=y_recv.at[cols - d - 1, z, p],
            **to_mode(member(lax.rem(col + d, cols), zq)))

    def got_y(d, z, p):
        peer = lax.rem(col + d, cols)
        part = gq.at[member(peer, z), pl.ds((p + 1) * comps, comps)]
        return pltpu.make_async_remote_copy(
            src_ref=part, dst_ref=part, send_sem=y_send.at[d - 1, z, p], recv_sem=y_recv.at[d - 1, z, p],
            **to_mode(member(peer, zq)))

    def copy_h(z, side):
        m = member(col, z)
        first, there, peer = ((nx * comps, 0, me + 1), (comps, (nx + 1) * comps, me + spaces - 1))[side]
        return pltpu.make_async_remote_copy(
            src_ref=gq.at[m, pl.ds(first, comps)], dst_ref=gq.at[m, pl.ds(there, comps)],
            send_sem=h_send.at[z, side], recv_sem=h_recv.at[z, side], **to_space(lax.rem(peer, spaces)))

    def copy_c(n):
        return pltpu.make_async_remote_copy(
            src_ref=cbo.at[n], dst_ref=crx.at[n],
            send_sem=c_send.at[n], recv_sem=c_recv.at[n], **to_space(row * 2 + 1 - core))

    def copy_s(n, d):
        peer = lax.rem(row + d, half)
        return pltpu.make_async_remote_copy(
            src_ref=xo.at[n, peer], dst_ref=xi.at[n, half - d - 1],
            send_sem=s_send.at[n, d - 1], recv_sem=s_recv.at[n, half - d - 1], **to_space(peer * 2 + core))

    def got_s(n, d):
        peer = lax.rem(row + d, half)
        return pltpu.make_async_remote_copy(
            src_ref=xo.at[n, peer], dst_ref=xi.at[n, d - 1],
            send_sem=s_send.at[n, d - 1], recv_sem=s_recv.at[n, d - 1], **to_space(peer * 2 + core))

    def copy_r(n):
        return pltpu.make_async_remote_copy(
            src_ref=zo.at[n], dst_ref=zi.at[n],
            send_sem=r_send.at[n], recv_sem=r_recv.at[n], **to_mode(member(col, lax.rem(zq + 1 + n // SPLIT, parts))))

    source = zq == parts - 1

    @pl.when(source)
    def _():
        for p in planes:
            for t in range(parts - 1):
                copy_z(t, p).start()

    for t in range(1, parts):
        @pl.when(t > zq)
        def _():
            for p in planes:
                copy_z(t, p).start()

    for p in planes:
        for d in range(1, cols):
            copy_y(d, zq, p).start()
    for side in range(2):
        copy_h(zq, side).start()

    for t in range(parts):
        edge = jnp.zeros((nm, lanes), F32)
        for u in range(units):
            low = roll(pk[(t - 1) % parts, u].astype(F32), 2 * u - width + 1)
            high = roll(pk[(t + 1) % parts, u].astype(F32), 2 * u + 1)
            edge = jnp.where(inner == 2 * u, low, jnp.where(inner == 2 * u + 1, high, edge))
        bd[t] = edge.astype(BF16)
    bq[zq] = bd[zq]
    for d in range(1, parts):
        copy_b(d).start()

    tail = zq == 0

    def other(n):
        head = parts - 1 if n == 0 else lax.rem(zq - n + parts - 1, parts - 1)
        return jnp.where(source, parts - 2 - n, head)

    adv_rel = cols - 1 - col

    def forward(z, p):
        got_z(z, p).wait_recv()
        for d in range(1, cols):
            copy_y(d, z, p).start()
        if p == nx - 1:
            copy_h(z, 0).start()
        if p == 0:
            copy_h(z, 1).start()

    def values_of(z, p):
        m = member(col, z)
        edge = bq[z].astype(F32)
        if p == 0:
            copy_h(z, 0).wait_recv()
        if p == nx - 1:
            copy_h(z, 1).wait_recv()
        grads = []
        for c in range(comps):
            u = p * comps + c
            at = (p + 1) * comps + c
            center = gq[m, at].astype(F32)
            gx = 0.5 * (gq[m, at + comps].astype(F32) - gq[m, at - comps].astype(F32))
            gy = 0.5 * (roll(center, -width) - roll(center, width))
            after = jnp.where(inner == width - 1, roll(edge, width - 2 - 2 * u), roll(center, -1))
            before = jnp.where(inner == 0, roll(edge, -2 * u), roll(center, 1))
            grads.append((gx, gy, 0.5 * (after - before)))

        def line(j, carry):
            rows = [jnp.broadcast_to(advf[p, d, pl.ds(j, 1), :], (nm, lanes)) for d in range(3)]
            start = pl.multiple_of(j * nm, nm)
            for c in range(comps):
                value = rows[0] * grads[c][0] + rows[1] * grads[c][1] + rows[2] * grads[c][2]
                vals[z, p * comps + c, pl.ds(start, nm), :] = value.astype(BF16)
            return carry

        lax.fori_loop(0, nm, line, 0, unroll=4)

    adv_rel = cols - 1 - col

    for p in planes:
        @pl.when(jnp.logical_not(source))
        def _():
            forward(other(0), p)
            if p == planes[0]:
                for t in range(parts - 2):
                    @pl.when(t < zq)
                    def _():
                        for k in planes:
                            copy_z(t, k).start()

        @pl.when(col != cols - 1)
        def _():
            got_y(adv_rel, parts - 1, p).wait_recv()

        for d in range(comps):
            advf[p, d] = gq[adv_block, (p + 1) * comps + d].astype(F32)
        values_of(zq, p)

        @pl.when(source)
        def _():
            forward(other(0), p)

        @pl.when(jnp.logical_not(tail))
        def _():
            forward(other(1), p)

    for n in range(parts - 1):
        got_b(other(n)).wait_recv()
        for p in planes:
            values_of(other(n), p)
            if n == 0:
                @pl.when(tail)
                def _():
                    forward(other(1), p)

                for k in range(2, parts - 1):
                    forward(other(k), p)

    for d in range(1, cols):
        for z in range(parts):
            def rest(d=d, z=z):
                for p in range(nx):
                    got_y(d, z, p).wait_recv()
            if z == parts - 1:
                pl.when(adv_rel != d)(rest)
            else:
                rest()

    for u in range(units):
        weight = wq[u // comps, 0:1, :]
        for t in range(NPANEL):
            for r in range(per_panel):
                raw = gq[plan_ref[1 + t] * per_panel + r, comps + u].astype(F32)
                first = (t * per_panel + r) * nm
                wts[u, first : first + nm, :] = (weight * raw).astype(BF16)

    def gemm(i):
        z = lax.rem(zq + 1 + i // SPLIT, parts)
        first = i % SPLIT * span
        left = jnp.concatenate([wts[u] for u in range(units)], axis=1)
        right = jnp.concatenate([vals[z, u, first : first + span] for u in range(units)], axis=1)
        part = lax.dot_general(left, right, (((1,), (1,)), ((), ())), preferred_element_type=F32)
        for s in range(spaces):
            acc[i, s % 2, s // 2] = part[s * own_rows : (s + 1) * own_rows]
        cbo[i] = acc[i, 1 - core].astype(BF16)
        copy_c(i).start()

    def stage_s(i):
        copy_c(i).wait_recv()
        for h in range(half):
            xo[i, h] = (acc[i, core, h] + crx[i, h].astype(F32)).astype(BF16)
        for d in range(1, half):
            copy_s(i, d).start()
        own[i] = acc[i, core, row] + crx[i, row].astype(F32)

    def total(i):
        value = own[i]
        for d in range(1, half):
            got_s(i, d).wait_recv()
            value = value + xi[i, d - 1].astype(F32)
        return value

    def stage_r(i):
        if i < steps - SPLIT:
            zo[i] = total(i).astype(BF16)
            copy_r(i).start()
        else:
            first = (i - steps + SPLIT) * span
            fin[:, first : first + span] = total(i)

    for i in range(steps + LAG_R):
        if i < steps:
            gemm(i)
        if LAG_S <= i < steps + LAG_S:
            stage_s(i - LAG_S)
        if i >= LAG_R:
            stage_r(i - LAG_R)

    for k in range(SPLIT):
        result = fin[:, k * span : (k + 1) * span]
        for n in range(parts - 1):
            copy_r(n * SPLIT + k).wait_recv()
            result = result + zi[n * SPLIT + k].astype(F32)
        fin[:, k * span : (k + 1) * span] = result
    for a in range(nm * nm // lanes):
        block = fin[:, a * lanes : (a + 1) * lanes]
        for e in range(lanes // nm):
            turned = pltpu.roll(block, lanes - e * nm, 1) if e else block
            out_ref[pl.ds(a * (lanes // nm) + e, own_rows, stride=nm), :] = turned[:, :nm]

    for t in range(parts):
        @pl.when(t != zq)
        def _():
            for p in range(nx):
                copy_z(t, p).wait_send()
    for d in range(1, parts):
        copy_b(d).wait_send()
    for z in range(parts):
        for d in range(1, cols):
            for p in range(nx):
                copy_y(d, z, p).wait_send()
        for side in range(2):
            copy_h(z, side).wait_send()
    for i in range(steps):
        copy_c(i).wait_send()
        for d in range(1, half):
            copy_s(i, d).wait_send()
        if i < steps - SPLIT:
            copy_r(i).wait_send()


def solution(mesh):
    nmode, spaces = mesh.shape["mode"], mesh.shape["space"]

    def local(modes, weights, plan):
        comps, nm, nx, cy, lanes = modes.shape
        parts, units = cy, comps * nx
        cols, half = nmode // parts, spaces // 2
        test_count = NPANEL * PANEL
        own_rows = test_count // spaces
        assert PANEL % nm == 0 and lanes % parts == 0 and 2 * units <= lanes // parts
        assert nmode % (2 * parts) == 0 and spaces % 2 == 0
        vm = pl.BlockSpec(memory_space=pltpu.VMEM)
        dma = pltpu.SemaphoreType.DMA
        steps = parts * SPLIT
        piece = (own_rows, nm * nm // SPLIT)
        pairs = max(half - 1, 1)
        out = pl.pallas_call(
            functools.partial(kernel, (nmode, spaces)),
            out_shape=jax.ShapeDtypeStruct((own_rows * nm, nm), F32),
            in_specs=[pl.BlockSpec(memory_space=pltpu.SMEM), vm, vm],
            out_specs=vm,
            scratch_shapes=[
                pltpu.VMEM((parts, units, nm, lanes), BF16),
                pltpu.VMEM((parts, nm, lanes), BF16),
                pltpu.VMEM((nmode, units + 2 * comps, nm, lanes), BF16),
                pltpu.VMEM((parts, nm, lanes), BF16),
                pltpu.VMEM((nx, 8, lanes), F32),
                pltpu.VMEM((nx, comps, nm, lanes), F32),
                pltpu.VMEM((units, test_count, lanes), BF16),
                pltpu.VMEM((parts, units, nm * nm, lanes), BF16),
                pltpu.VMEM((steps, 2, half) + piece, F32),
                pltpu.VMEM((steps, half) + piece, BF16),
                pltpu.VMEM((steps, half) + piece, BF16),
                pltpu.VMEM((steps,) + piece, F32),
                pltpu.VMEM((steps, half) + piece, BF16),
                pltpu.VMEM((steps, pairs) + piece, BF16),
                pltpu.VMEM((steps - SPLIT,) + piece, BF16),
                pltpu.VMEM((steps - SPLIT,) + piece, BF16),
                pltpu.VMEM((own_rows, nm * nm), F32),
                dma((parts, nx)), dma((parts, nx)), dma((parts - 1,)), dma((parts,)),
                dma((cols - 1, parts, nx)), dma((cols - 1, parts, nx)), dma((parts, 2)), dma((parts, 2)),
                dma((steps,)), dma((steps,)), dma((steps, pairs)), dma((steps, pairs)),
                dma((steps - SPLIT,)), dma((steps - SPLIT,)),
            ],
            compiler_params=pltpu.CompilerParams(
                collective_id=0, has_side_effects=True, vmem_limit_bytes=56 * 1024 * 1024),
        )(plan, modes, weights)
        return out.reshape(own_rows, nm, nm)

    in_specs = (P(None, "mode", "space", None, None), P("space", None, None), P())
    return jax.shard_map(local, mesh=mesh, in_specs=in_specs, out_specs=P("space", None, "mode"), check_vma=False)
```

```python
import functools

import jax
import jax.numpy as jnp
from jax import lax
from jax.experimental import pallas as pl
from jax.experimental.pallas import tpu as pltpu
from jax.sharding import PartitionSpec as P

PANEL = 64
NPANEL = 2
SPLIT = 2
LAG_S = 2
LAG_R = 7
MESH = pl.DeviceIdType.MESH
F32 = jnp.float32
BF16 = jnp.bfloat16


def kernel(dims, plan_ref, x_ref, weights_ref, out_ref,
           pk, bd, gq, bq, wq, advf, wts, vals, acc, cbo, crx, own, xo, xi, zo, zi, fin,
           z_send, z_recv, b_send, b_recv, y_send, y_recv, h_send, h_recv,
           c_send, c_recv, s_send, s_recv, r_send, r_recv):
    nmode, spaces = dims
    comps, nm, nx, cy, lanes = x_ref.shape
    own_rows = out_ref.shape[0] // nm
    parts = cy
    width = lanes // parts
    units = nx * comps
    cols = nmode // parts
    half = spaces // 2
    per_panel = PANEL // nm
    mode = lax.axis_index("mode")
    me = lax.axis_index("space")
    zq = lax.rem(mode // 2, parts)
    col = (mode // (2 * parts)) * 2 + lax.rem(mode, 2)
    core = lax.rem(me, 2)
    row = me // 2
    adv_block = nmode - 1
    planes = list(range(1, nx - 1)) + [0, nx - 1]
    steps = parts * SPLIT
    span = nm * nm // SPLIT

    def member(c, z):
        return (c // 2) * (2 * parts) + z * 2 + lax.rem(c, 2)

    def to_mode(m):
        return {"device_id": {"mode": m}, "device_id_type": MESH}

    def to_space(s):
        return {"device_id": {"space": s}, "device_id_type": MESH}

    barrier = pltpu.get_barrier_semaphore()
    for d in range(1, parts):
        pl.semaphore_signal(barrier, inc=1, **to_mode(member(col, lax.rem(zq + d, parts))))
    for d in range(1, cols):
        pl.semaphore_signal(barrier, inc=1, **to_mode(member(lax.rem(col + d, cols), zq)))
    for d in range(1, spaces):
        pl.semaphore_signal(barrier, inc=1, **to_space(lax.rem(me + d, spaces)))

    lane = lax.broadcasted_iota(jnp.int32, (nm, lanes), 1)
    group, inner = lane // width, lax.rem(lane, width)

    def roll(v, shift):
        shift = shift % lanes
        return pltpu.roll(v, shift, 1) if shift else v

    for p in range(nx):
        for c in range(comps):
            u = p * comps + c
            rows = jnp.swapaxes(x_ref[c, :, p], 0, 1)
            rows = [rows[y].astype(F32) for y in range(cy)]
            for t in range(parts):
                v = roll(rows[0], -width * t)
                for y in range(1, cy):
                    v = jnp.where(group == y, roll(rows[y], width * (y - t)), v)
                pk[t, u] = v.astype(BF16)
    gq[mode, comps : comps + units] = pk[zq]
    for p in range(nx):
        w = None
        for y in range(cy):
            line = jnp.broadcast_to(weights_ref[p, y : y + 1, :], (8, lanes))
            line = pltpu.roll(line, lax.rem(width * (y - zq + parts), lanes), 1)
            w = line if w is None else jnp.where(group[:8] == y, line, w)
        wq[p] = w

    pl.semaphore_wait(barrier, parts - 1 + cols - 1 + spaces - 1)

    def copy_z(t, p):
        return pltpu.make_async_remote_copy(
            src_ref=pk.at[t, pl.ds(p * comps, comps)], dst_ref=gq.at[mode, pl.ds((p + 1) * comps, comps)],
            send_sem=z_send.at[t, p], recv_sem=z_recv.at[zq, p], **to_mode(member(col, t)))

    def got_z(z, p):
        m = member(col, z)
        return pltpu.make_async_remote_copy(
            src_ref=pk.at[0, pl.ds(p * comps, comps)], dst_ref=gq.at[m, pl.ds((p + 1) * comps, comps)],
            send_sem=z_send.at[0, p], recv_sem=z_recv.at[z, p], **to_mode(m))

    def copy_b(d):
        t = lax.rem(zq + d, parts)
        return pltpu.make_async_remote_copy(
            src_ref=bd.at[t], dst_ref=bq.at[zq],
            send_sem=b_send.at[d - 1], recv_sem=b_recv.at[zq], **to_mode(member(col, t)))

    def got_b(z):
        return pltpu.make_async_remote_copy(
            src_ref=bd.at[0], dst_ref=bq.at[z],
            send_sem=b_send.at[0], recv_sem=b_recv.at[z], **to_mode(member(col, z)))

    def copy_y(d, z, p):
        m = member(col, z)
        part = gq.at[m, pl.ds((p + 1) * comps, comps)]
        return pltpu.make_async_remote_copy(
            src_ref=part, dst_ref=part, send_sem=y_send.at[d - 1, z, p], recv_sem=y_recv.at[cols - d - 1, z, p],
            **to_mode(member(lax.rem(col + d, cols), zq)))

    def got_y(d, z, p):
        peer = lax.rem(col + d, cols)
        part = gq.at[member(peer, z), pl.ds((p + 1) * comps, comps)]
        return pltpu.make_async_remote_copy(
            src_ref=part, dst_ref=part, send_sem=y_send.at[d - 1, z, p], recv_sem=y_recv.at[d - 1, z, p],
            **to_mode(member(peer, zq)))

    def copy_h(z, side):
        m = member(col, z)
        first, there, peer = ((nx * comps, 0, me + 1), (comps, (nx + 1) * comps, me + spaces - 1))[side]
        return pltpu.make_async_remote_copy(
            src_ref=gq.at[m, pl.ds(first, comps)], dst_ref=gq.at[m, pl.ds(there, comps)],
            send_sem=h_send.at[z, side], recv_sem=h_recv.at[z, side], **to_space(lax.rem(peer, spaces)))

    def copy_c(n):
        return pltpu.make_async_remote_copy(
            src_ref=cbo.at[n], dst_ref=crx.at[n],
            send_sem=c_send.at[n], recv_sem=c_recv.at[n], **to_space(row * 2 + 1 - core))

    def copy_s(n, d):
        peer = lax.rem(row + d, half)
        return pltpu.make_async_remote_copy(
            src_ref=xo.at[n, peer], dst_ref=xi.at[n, half - d - 1],
            send_sem=s_send.at[n, d - 1], recv_sem=s_recv.at[n, half - d - 1], **to_space(peer * 2 + core))

    def got_s(n, d):
        peer = lax.rem(row + d, half)
        return pltpu.make_async_remote_copy(
            src_ref=xo.at[n, peer], dst_ref=xi.at[n, d - 1],
            send_sem=s_send.at[n, d - 1], recv_sem=s_recv.at[n, d - 1], **to_space(peer * 2 + core))

    def copy_r(n):
        return pltpu.make_async_remote_copy(
            src_ref=zo.at[n], dst_ref=zi.at[n],
            send_sem=r_send.at[n], recv_sem=r_recv.at[n], **to_mode(member(col, lax.rem(zq + 1 + n // SPLIT, parts))))

    source = zq == parts - 1

    @pl.when(source)
    def _():
        for p in planes:
            for t in range(parts - 1):
                copy_z(t, p).start()

    for t in range(1, parts):
        @pl.when(t > zq)
        def _():
            for p in planes:
                copy_z(t, p).start()

    for p in planes:
        for d in range(1, cols):
            copy_y(d, zq, p).start()
    for side in range(2):
        copy_h(zq, side).start()

    for t in range(parts):
        edge = jnp.zeros((nm, lanes), F32)
        for u in range(units):
            low = roll(pk[(t - 1) % parts, u].astype(F32), 2 * u - width + 1)
            high = roll(pk[(t + 1) % parts, u].astype(F32), 2 * u + 1)
            edge = jnp.where(inner == 2 * u, low, jnp.where(inner == 2 * u + 1, high, edge))
        bd[t] = edge.astype(BF16)
    bq[zq] = bd[zq]
    for d in range(1, parts):
        copy_b(d).start()

    def other(n):
        head = parts - 1 if n == 0 else lax.rem(zq - n + parts - 1, parts - 1)
        return jnp.where(source, parts - 2 - n, head)

    adv_rel = cols - 1 - col

    def forward(z, p):
        got_z(z, p).wait_recv()
        for d in range(1, cols):
            copy_y(d, z, p).start()
        if p == nx - 1:
            copy_h(z, 0).start()
        if p == 0:
            copy_h(z, 1).start()

    def values_of(z, p):
        m = member(col, z)
        edge = bq[z].astype(F32)
        if p == 0:
            copy_h(z, 0).wait_recv()
        if p == nx - 1:
            copy_h(z, 1).wait_recv()
        grads = []
        for c in range(comps):
            u = p * comps + c
            at = (p + 1) * comps + c
            center = gq[m, at].astype(F32)
            gx = 0.5 * (gq[m, at + comps].astype(F32) - gq[m, at - comps].astype(F32))
            gy = 0.5 * (roll(center, -width) - roll(center, width))
            after = jnp.where(inner == width - 1, roll(edge, width - 2 - 2 * u), roll(center, -1))
            before = jnp.where(inner == 0, roll(edge, -2 * u), roll(center, 1))
            grads.append((gx, gy, 0.5 * (after - before)))

        def line(j, carry):
            rows = [jnp.broadcast_to(advf[p, d, pl.ds(j, 1), :], (nm, lanes)) for d in range(3)]
            start = pl.multiple_of(j * nm, nm)
            for c in range(comps):
                value = rows[0] * grads[c][0] + rows[1] * grads[c][1] + rows[2] * grads[c][2]
                vals[z, p * comps + c, pl.ds(start, nm), :] = value.astype(BF16)
            return carry

        lax.fori_loop(0, nm, line, 0, unroll=4)

    adv_rel = cols - 1 - col

    for p in planes:
        @pl.when(jnp.logical_not(source))
        def _():
            at = planes.index(p)
            for k in planes[:2] if at == 0 else planes[at + 1 : at + 2]:
                forward(other(0), k)
                if k == planes[0]:
                    for t in range(parts - 2):
                        @pl.when(t < zq)
                        def _():
                            for r in planes:
                                copy_z(t, r).start()

        @pl.when(col != cols - 1)
        def _():
            got_y(adv_rel, parts - 1, p).wait_recv()

        for d in range(comps):
            advf[p, d] = gq[adv_block, (p + 1) * comps + d].astype(F32)
        values_of(zq, p)

        @pl.when(source)
        def _():
            forward(other(0), p)

    for n in range(parts - 1):
        got_b(other(n)).wait_recv()
        for p in planes:
            values_of(other(n), p)
            if n == 0:
                for k in range(1, parts - 1):
                    forward(other(k), p)

    for d in range(1, cols):
        for z in range(parts):
            def rest(d=d, z=z):
                for p in range(nx):
                    got_y(d, z, p).wait_recv()
            if z == parts - 1:
                pl.when(adv_rel != d)(rest)
            else:
                rest()

    for u in range(units):
        weight = wq[u // comps, 0:1, :]
        for t in range(NPANEL):
            for r in range(per_panel):
                raw = gq[plan_ref[1 + t] * per_panel + r, comps + u].astype(F32)
                first = (t * per_panel + r) * nm
                wts[u, first : first + nm, :] = (weight * raw).astype(BF16)

    def gemm(i):
        z = lax.rem(zq + 1 + i // SPLIT, parts)
        first = i % SPLIT * span
        left = jnp.concatenate([wts[u] for u in range(units)], axis=1)
        right = jnp.concatenate([vals[z, u, first : first + span] for u in range(units)], axis=1)
        part = lax.dot_general(left, right, (((1,), (1,)), ((), ())), preferred_element_type=F32)
        for s in range(spaces):
            acc[i, s % 2, s // 2] = part[s * own_rows : (s + 1) * own_rows]
        cbo[i] = acc[i, 1 - core].astype(BF16)
        copy_c(i).start()

    def stage_s(i):
        copy_c(i).wait_recv()
        for h in range(half):
            xo[i, h] = (acc[i, core, h] + crx[i, h].astype(F32)).astype(BF16)
        for d in range(1, half):
            copy_s(i, d).start()
        own[i] = acc[i, core, row] + crx[i, row].astype(F32)

    def total(i):
        value = own[i]
        for d in range(1, half):
            got_s(i, d).wait_recv()
            value = value + xi[i, d - 1].astype(F32)
        return value

    def stage_r(i):
        if i < steps - SPLIT:
            zo[i] = total(i).astype(BF16)
            copy_r(i).start()
        else:
            first = (i - steps + SPLIT) * span
            fin[:, first : first + span] = total(i)

    for i in range(steps + LAG_R):
        if i < steps:
            gemm(i)
        if LAG_S <= i < steps + LAG_S:
            stage_s(i - LAG_S)
        if i >= LAG_R:
            stage_r(i - LAG_R)

    for k in range(SPLIT):
        result = fin[:, k * span : (k + 1) * span]
        for n in range(parts - 1):
            copy_r(n * SPLIT + k).wait_recv()
            result = result + zi[n * SPLIT + k].astype(F32)
        fin[:, k * span : (k + 1) * span] = result
    for a in range(nm * nm // lanes):
        block = fin[:, a * lanes : (a + 1) * lanes]
        for e in range(lanes // nm):
            turned = pltpu.roll(block, lanes - e * nm, 1) if e else block
            out_ref[pl.ds(a * (lanes // nm) + e, own_rows, stride=nm), :] = turned[:, :nm]

    for t in range(parts):
        @pl.when(t != zq)
        def _():
            for p in range(nx):
                copy_z(t, p).wait_send()
    for d in range(1, parts):
        copy_b(d).wait_send()
    for z in range(parts):
        for d in range(1, cols):
            for p in range(nx):
                copy_y(d, z, p).wait_send()
        for side in range(2):
            copy_h(z, side).wait_send()
    for i in range(steps):
        copy_c(i).wait_send()
        for d in range(1, half):
            copy_s(i, d).wait_send()
        if i < steps - SPLIT:
            copy_r(i).wait_send()


def solution(mesh):
    nmode, spaces = mesh.shape["mode"], mesh.shape["space"]

    def local(modes, weights, plan):
        comps, nm, nx, cy, lanes = modes.shape
        parts, units = cy, comps * nx
        cols, half = nmode // parts, spaces // 2
        test_count = NPANEL * PANEL
        own_rows = test_count // spaces
        assert PANEL % nm == 0 and lanes % parts == 0 and 2 * units <= lanes // parts
        assert nmode % (2 * parts) == 0 and spaces % 2 == 0
        vm = pl.BlockSpec(memory_space=pltpu.VMEM)
        dma = pltpu.SemaphoreType.DMA
        steps = parts * SPLIT
        piece = (own_rows, nm * nm // SPLIT)
        pairs = max(half - 1, 1)
        out = pl.pallas_call(
            functools.partial(kernel, (nmode, spaces)),
            out_shape=jax.ShapeDtypeStruct((own_rows * nm, nm), F32),
            in_specs=[pl.BlockSpec(memory_space=pltpu.SMEM), vm, vm],
            out_specs=vm,
            scratch_shapes=[
                pltpu.VMEM((parts, units, nm, lanes), BF16),
                pltpu.VMEM((parts, nm, lanes), BF16),
                pltpu.VMEM((nmode, units + 2 * comps, nm, lanes), BF16),
                pltpu.VMEM((parts, nm, lanes), BF16),
                pltpu.VMEM((nx, 8, lanes), F32),
                pltpu.VMEM((nx, comps, nm, lanes), F32),
                pltpu.VMEM((units, test_count, lanes), BF16),
                pltpu.VMEM((parts, units, nm * nm, lanes), BF16),
                pltpu.VMEM((steps, 2, half) + piece, F32),
                pltpu.VMEM((steps, half) + piece, BF16),
                pltpu.VMEM((steps, half) + piece, BF16),
                pltpu.VMEM((steps,) + piece, F32),
                pltpu.VMEM((steps, half) + piece, BF16),
                pltpu.VMEM((steps, pairs) + piece, BF16),
                pltpu.VMEM((steps - SPLIT,) + piece, BF16),
                pltpu.VMEM((steps - SPLIT,) + piece, BF16),
                pltpu.VMEM((own_rows, nm * nm), F32),
                dma((parts, nx)), dma((parts, nx)), dma((parts - 1,)), dma((parts,)),
                dma((cols - 1, parts, nx)), dma((cols - 1, parts, nx)), dma((parts, 2)), dma((parts, 2)),
                dma((steps,)), dma((steps,)), dma((steps, pairs)), dma((steps, pairs)),
                dma((steps - SPLIT,)), dma((steps - SPLIT,)),
            ],
            compiler_params=pltpu.CompilerParams(
                collective_id=0, has_side_effects=True, vmem_limit_bytes=56 * 1024 * 1024),
        )(plan, modes, weights)
        return out.reshape(own_rows, nm, nm)

    in_specs = (P(None, "mode", "space", None, None), P("space", None, None), P())
    return jax.shard_map(local, mesh=mesh, in_specs=in_specs, out_specs=P("space", None, "mode"), check_vma=False)
```

```python
import functools

import jax
import jax.numpy as jnp
from jax import lax
from jax.experimental import pallas as pl
from jax.experimental.pallas import tpu as pltpu
from jax.sharding import PartitionSpec as P

PANEL = 64
NPANEL = 2
SPLIT = 2
LAG_S = 2
LAG_R = 7
MESH = pl.DeviceIdType.MESH
F32 = jnp.float32
BF16 = jnp.bfloat16


def kernel(dims, plan_ref, x_ref, weights_ref, out_ref,
           pk, bd, gq, bq, wq, advf, wts, vals, acc, cbo, crx, own, xo, xi, zo, zi, fin,
           z_send, z_recv, b_send, b_recv, y_send, y_recv, h_send, h_recv,
           c_send, c_recv, s_send, s_recv, r_send, r_recv):
    nmode, spaces = dims
    comps, nm, nx, cy, lanes = x_ref.shape
    own_rows = out_ref.shape[0] // nm
    parts = cy
    width = lanes // parts
    units = nx * comps
    cols = nmode // parts
    half = spaces // 2
    per_panel = PANEL // nm
    mode = lax.axis_index("mode")
    me = lax.axis_index("space")
    zq = lax.rem(mode // 2, parts)
    col = (mode // (2 * parts)) * 2 + lax.rem(mode, 2)
    core = lax.rem(me, 2)
    row = me // 2
    adv_block = nmode - 1
    planes = list(range(1, nx - 1)) + [0, nx - 1]
    steps = parts * SPLIT
    span = nm * nm // SPLIT

    def member(c, z):
        return (c // 2) * (2 * parts) + z * 2 + lax.rem(c, 2)

    def to_mode(m):
        return {"device_id": {"mode": m}, "device_id_type": MESH}

    def to_space(s):
        return {"device_id": {"space": s}, "device_id_type": MESH}

    barrier = pltpu.get_barrier_semaphore()
    for d in range(1, parts):
        pl.semaphore_signal(barrier, inc=1, **to_mode(member(col, lax.rem(zq + d, parts))))
    for d in range(1, cols):
        pl.semaphore_signal(barrier, inc=1, **to_mode(member(lax.rem(col + d, cols), zq)))
    for d in range(1, spaces):
        pl.semaphore_signal(barrier, inc=1, **to_space(lax.rem(me + d, spaces)))

    lane = lax.broadcasted_iota(jnp.int32, (nm, lanes), 1)
    group, inner = lane // width, lax.rem(lane, width)

    def roll(v, shift):
        shift = shift % lanes
        return pltpu.roll(v, shift, 1) if shift else v

    for p in range(nx):
        for c in range(comps):
            u = p * comps + c
            rows = jnp.swapaxes(x_ref[c, :, p], 0, 1)
            rows = [rows[y].astype(F32) for y in range(cy)]
            for t in range(parts):
                v = roll(rows[0], -width * t)
                for y in range(1, cy):
                    v = jnp.where(group == y, roll(rows[y], width * (y - t)), v)
                pk[t, u] = v.astype(BF16)
    gq[mode, comps : comps + units] = pk[zq]
    for p in range(nx):
        w = None
        for y in range(cy):
            line = jnp.broadcast_to(weights_ref[p, y : y + 1, :], (8, lanes))
            line = pltpu.roll(line, lax.rem(width * (y - zq + parts), lanes), 1)
            w = line if w is None else jnp.where(group[:8] == y, line, w)
        wq[p] = w

    pl.semaphore_wait(barrier, parts - 1 + cols - 1 + spaces - 1)

    def copy_z(t, p):
        return pltpu.make_async_remote_copy(
            src_ref=pk.at[t, pl.ds(p * comps, comps)], dst_ref=gq.at[mode, pl.ds((p + 1) * comps, comps)],
            send_sem=z_send.at[t, p], recv_sem=z_recv.at[zq, p], **to_mode(member(col, t)))

    def got_z(z, p):
        m = member(col, z)
        return pltpu.make_async_remote_copy(
            src_ref=pk.at[0, pl.ds(p * comps, comps)], dst_ref=gq.at[m, pl.ds((p + 1) * comps, comps)],
            send_sem=z_send.at[0, p], recv_sem=z_recv.at[z, p], **to_mode(m))

    def copy_b(d):
        t = lax.rem(zq + d, parts)
        return pltpu.make_async_remote_copy(
            src_ref=bd.at[t], dst_ref=bq.at[zq],
            send_sem=b_send.at[d - 1], recv_sem=b_recv.at[zq], **to_mode(member(col, t)))

    def got_b(z):
        return pltpu.make_async_remote_copy(
            src_ref=bd.at[0], dst_ref=bq.at[z],
            send_sem=b_send.at[0], recv_sem=b_recv.at[z], **to_mode(member(col, z)))

    def copy_y(d, z, p):
        m = member(col, z)
        part = gq.at[m, pl.ds((p + 1) * comps, comps)]
        return pltpu.make_async_remote_copy(
            src_ref=part, dst_ref=part, send_sem=y_send.at[d - 1, z, p], recv_sem=y_recv.at[cols - d - 1, z, p],
            **to_mode(member(lax.rem(col + d, cols), zq)))

    def got_y(d, z, p):
        peer = lax.rem(col + d, cols)
        part = gq.at[member(peer, z), pl.ds((p + 1) * comps, comps)]
        return pltpu.make_async_remote_copy(
            src_ref=part, dst_ref=part, send_sem=y_send.at[d - 1, z, p], recv_sem=y_recv.at[d - 1, z, p],
            **to_mode(member(peer, zq)))

    def copy_h(z, side):
        m = member(col, z)
        first, there, peer = ((nx * comps, 0, me + 1), (comps, (nx + 1) * comps, me + spaces - 1))[side]
        return pltpu.make_async_remote_copy(
            src_ref=gq.at[m, pl.ds(first, comps)], dst_ref=gq.at[m, pl.ds(there, comps)],
            send_sem=h_send.at[z, side], recv_sem=h_recv.at[z, side], **to_space(lax.rem(peer, spaces)))

    def copy_c(n):
        return pltpu.make_async_remote_copy(
            src_ref=cbo.at[n], dst_ref=crx.at[n],
            send_sem=c_send.at[n], recv_sem=c_recv.at[n], **to_space(row * 2 + 1 - core))

    def copy_s(n, d):
        peer = lax.rem(row + d, half)
        return pltpu.make_async_remote_copy(
            src_ref=xo.at[n, peer], dst_ref=xi.at[n, half - d - 1],
            send_sem=s_send.at[n, d - 1], recv_sem=s_recv.at[n, half - d - 1], **to_space(peer * 2 + core))

    def got_s(n, d):
        peer = lax.rem(row + d, half)
        return pltpu.make_async_remote_copy(
            src_ref=xo.at[n, peer], dst_ref=xi.at[n, d - 1],
            send_sem=s_send.at[n, d - 1], recv_sem=s_recv.at[n, d - 1], **to_space(peer * 2 + core))

    def copy_r(n):
        return pltpu.make_async_remote_copy(
            src_ref=zo.at[n], dst_ref=zi.at[n],
            send_sem=r_send.at[n], recv_sem=r_recv.at[n], **to_mode(member(col, lax.rem(zq + 1 + n // SPLIT, parts))))

    source = zq == parts - 1

    @pl.when(source)
    def _():
        for p in planes:
            for t in range(parts - 1):
                copy_z(t, p).start()

    for t in range(1, parts):
        @pl.when(t > zq)
        def _():
            for p in planes:
                copy_z(t, p).start()

    for p in planes:
        for d in range(1, cols):
            copy_y(d, zq, p).start()
    for side in range(2):
        copy_h(zq, side).start()

    for t in range(parts):
        edge = jnp.zeros((nm, lanes), F32)
        for u in range(units):
            low = roll(pk[(t - 1) % parts, u].astype(F32), 2 * u - width + 1)
            high = roll(pk[(t + 1) % parts, u].astype(F32), 2 * u + 1)
            edge = jnp.where(inner == 2 * u, low, jnp.where(inner == 2 * u + 1, high, edge))
        bd[t] = edge.astype(BF16)
    bq[zq] = bd[zq]
    for d in range(1, parts):
        copy_b(d).start()

    def other(n):
        head = parts - 1 if n == 0 else lax.rem(zq - n + parts - 1, parts - 1)
        return jnp.where(source, parts - 2 - n, head)

    adv_rel = cols - 1 - col

    def forward(z, p):
        got_z(z, p).wait_recv()
        for d in range(1, cols):
            copy_y(d, z, p).start()
        if p == nx - 1:
            copy_h(z, 0).start()
        if p == 0:
            copy_h(z, 1).start()

    def values_of(z, p):
        m = member(col, z)
        edge = bq[z].astype(F32)
        if p == 0:
            copy_h(z, 0).wait_recv()
        if p == nx - 1:
            copy_h(z, 1).wait_recv()
        grads = []
        for c in range(comps):
            u = p * comps + c
            at = (p + 1) * comps + c
            center = gq[m, at].astype(F32)
            gx = 0.5 * (gq[m, at + comps].astype(F32) - gq[m, at - comps].astype(F32))
            gy = 0.5 * (roll(center, -width) - roll(center, width))
            after = jnp.where(inner == width - 1, roll(edge, width - 2 - 2 * u), roll(center, -1))
            before = jnp.where(inner == 0, roll(edge, -2 * u), roll(center, 1))
            grads.append((gx, gy, 0.5 * (after - before)))

        def line(j, carry):
            rows = [jnp.broadcast_to(advf[p, d, pl.ds(j, 1), :], (nm, lanes)) for d in range(3)]
            start = pl.multiple_of(j * nm, nm)
            for c in range(comps):
                value = rows[0] * grads[c][0] + rows[1] * grads[c][1] + rows[2] * grads[c][2]
                vals[z, p * comps + c, pl.ds(start, nm), :] = value.astype(BF16)
            return carry

        lax.fori_loop(0, nm, line, 0, unroll=4)

    adv_rel = cols - 1 - col

    for p in planes:
        @pl.when(jnp.logical_not(source))
        def _():
            at = planes.index(p)
            for k in planes[:2] if at == 0 else planes[at + 1 : at + 2]:
                forward(other(0), k)
                if k == planes[0]:
                    for t in range(parts - 2):
                        @pl.when(t < zq)
                        def _():
                            for r in planes:
                                copy_z(t, r).start()

        @pl.when(col != cols - 1)
        def _():
            got_y(adv_rel, parts - 1, p).wait_recv()

        for d in range(comps):
            advf[p, d] = gq[adv_block, (p + 1) * comps + d].astype(F32)
        values_of(zq, p)

        @pl.when(source)
        def _():
            forward(other(0), p)

    for n in range(parts - 1):
        got_b(other(n)).wait_recv()
        for p in planes:
            values_of(other(n), p)
            if n == 0:
                for k in range(1, parts - 1):
                    forward(other(k), p)

    for d in range(1, cols):
        for z in range(parts):
            def rest(d=d, z=z):
                for p in range(nx):
                    got_y(d, z, p).wait_recv()
            if z == parts - 1:
                pl.when(adv_rel != d)(rest)
            else:
                rest()

    for u in range(units):
        weight = wq[u // comps, 0:1, :]
        for t in range(NPANEL):
            for r in range(per_panel):
                raw = gq[plan_ref[1 + t] * per_panel + r, comps + u].astype(F32)
                first = (t * per_panel + r) * nm
                wts[u, first : first + nm, :] = (weight * raw).astype(BF16)

    def gemm(i):
        z = lax.rem(zq + 1 + i // SPLIT, parts)
        first = i % SPLIT * span
        left = jnp.concatenate([wts[u] for u in range(units)], axis=1)
        right = jnp.concatenate([vals[z, u, first : first + span] for u in range(units)], axis=1)
        part = lax.dot_general(left, right, (((1,), (1,)), ((), ())), preferred_element_type=F32)
        for s in range(spaces):
            acc[i, s % 2, s // 2] = part[s * own_rows : (s + 1) * own_rows]
        cbo[i] = acc[i, 1 - core].astype(BF16)
        copy_c(i).start()

    def stage_s(i):
        copy_c(i).wait_recv()
        for h in range(half):
            xo[i, h] = (acc[i, core, h] + crx[i, h].astype(F32)).astype(BF16)
        for d in range(1, half):
            copy_s(i, d).start()
        own[i] = acc[i, core, row] + crx[i, row].astype(F32)

    def total(i):
        value = own[i]
        for d in range(1, half):
            got_s(i, d).wait_recv()
            value = value + xi[i, d - 1].astype(F32)
        return value

    def finish(k):
        first = k * span
        for n in range(parts - 1):
            copy_r(n * SPLIT + k).wait_recv()
        arrived = zi[k].astype(F32)
        for n in range(1, parts - 1):
            arrived = arrived + zi[n * SPLIT + k].astype(F32)
        fin[:, first : first + span] = arrived
        fin[:, first : first + span] += total(steps - SPLIT + k)
        for a in range(first // lanes, (first + span) // lanes):
            block = fin[:, a * lanes : (a + 1) * lanes]
            for e in range(lanes // nm):
                turned = pltpu.roll(block, lanes - e * nm, 1) if e else block
                out_ref[pl.ds(a * (lanes // nm) + e, own_rows, stride=nm), :] = turned[:, :nm]

    def stage_r(i):
        if i < steps - SPLIT:
            zo[i] = total(i).astype(BF16)
            copy_r(i).start()
        else:
            finish(i - steps + SPLIT)

    for i in range(steps + LAG_R):
        if i < steps:
            gemm(i)
        if LAG_S <= i < steps + LAG_S:
            stage_s(i - LAG_S)
        if i >= LAG_R:
            stage_r(i - LAG_R)

    for t in range(parts):
        @pl.when(t != zq)
        def _():
            for p in range(nx):
                copy_z(t, p).wait_send()
    for d in range(1, parts):
        copy_b(d).wait_send()
    for z in range(parts):
        for d in range(1, cols):
            for p in range(nx):
                copy_y(d, z, p).wait_send()
        for side in range(2):
            copy_h(z, side).wait_send()
    for i in range(steps):
        copy_c(i).wait_send()
        for d in range(1, half):
            copy_s(i, d).wait_send()
        if i < steps - SPLIT:
            copy_r(i).wait_send()


def solution(mesh):
    nmode, spaces = mesh.shape["mode"], mesh.shape["space"]

    def local(modes, weights, plan):
        comps, nm, nx, cy, lanes = modes.shape
        parts, units = cy, comps * nx
        cols, half = nmode // parts, spaces // 2
        test_count = NPANEL * PANEL
        own_rows = test_count // spaces
        assert PANEL % nm == 0 and lanes % parts == 0 and 2 * units <= lanes // parts
        assert nmode % (2 * parts) == 0 and spaces % 2 == 0
        vm = pl.BlockSpec(memory_space=pltpu.VMEM)
        dma = pltpu.SemaphoreType.DMA
        steps = parts * SPLIT
        piece = (own_rows, nm * nm // SPLIT)
        pairs = max(half - 1, 1)
        out = pl.pallas_call(
            functools.partial(kernel, (nmode, spaces)),
            out_shape=jax.ShapeDtypeStruct((own_rows * nm, nm), F32),
            in_specs=[pl.BlockSpec(memory_space=pltpu.SMEM), vm, vm],
            out_specs=vm,
            scratch_shapes=[
                pltpu.VMEM((parts, units, nm, lanes), BF16),
                pltpu.VMEM((parts, nm, lanes), BF16),
                pltpu.VMEM((nmode, units + 2 * comps, nm, lanes), BF16),
                pltpu.VMEM((parts, nm, lanes), BF16),
                pltpu.VMEM((nx, 8, lanes), F32),
                pltpu.VMEM((nx, comps, nm, lanes), F32),
                pltpu.VMEM((units, test_count, lanes), BF16),
                pltpu.VMEM((parts, units, nm * nm, lanes), BF16),
                pltpu.VMEM((steps, 2, half) + piece, F32),
                pltpu.VMEM((steps, half) + piece, BF16),
                pltpu.VMEM((steps, half) + piece, BF16),
                pltpu.VMEM((steps,) + piece, F32),
                pltpu.VMEM((steps, half) + piece, BF16),
                pltpu.VMEM((steps, pairs) + piece, BF16),
                pltpu.VMEM((steps - SPLIT,) + piece, BF16),
                pltpu.VMEM((steps - SPLIT,) + piece, BF16),
                pltpu.VMEM((own_rows, nm * nm), F32),
                dma((parts, nx)), dma((parts, nx)), dma((parts - 1,)), dma((parts,)),
                dma((cols - 1, parts, nx)), dma((cols - 1, parts, nx)), dma((parts, 2)), dma((parts, 2)),
                dma((steps,)), dma((steps,)), dma((steps, pairs)), dma((steps, pairs)),
                dma((steps - SPLIT,)), dma((steps - SPLIT,)),
            ],
            compiler_params=pltpu.CompilerParams(
                collective_id=0, has_side_effects=True, vmem_limit_bytes=56 * 1024 * 1024),
        )(plan, modes, weights)
        return out.reshape(own_rows, nm, nm)

    in_specs = (P(None, "mode", "space", None, None), P("space", None, None), P())
    return jax.shard_map(local, mesh=mesh, in_specs=in_specs, out_specs=P("space", None, "mode"), check_vma=False)
```
